32 devices in a mesh: rep: 2 (over y), grp: 2 (over core), blk: 8 (over z, x).
Axes of the slice: x: 2, y: 2, z: 4, core: 2. Of those that a mesh axis runs over, the one named last changes fastest.
Arguments:
- queries: bfloat16 [2048, 8, 576], P(('rep', 'grp'), 'blk'), parts along dimension 0, may hold values from -64 to 64
- latents: bfloat16 [2048, 576], P(('rep', 'grp', 'blk')), parts along dimension 0, may hold values from -12 to 12
- out_grad: bfloat16 [2048, 8, 512], P(('rep', 'grp'), 'blk'), parts along dimension 0, may hold values from -6 to 6
- first_key: int32 [2048], P(('rep', 'grp')), parts along dimension 0, may hold values from 0 to 127, as said below
Outputs:
- query_grad: bfloat16 [2048, 8, 576], P(('rep', 'grp'), 'blk'), parts along dimension 0
- latent_grad: bfloat16 [2048, 576], P(('rep', 'grp', 'blk')), parts along dimension 0
The draws below stay inside these ranges and needn't reach their ends.
There are 2 independent parts, one for each index of `rep`. The reference program is written for one: setup_inputs(seed, part) draws one part's arguments, and reference() takes and returns one part's arrays. A program takes and returns all parts, laid end to end along the dimension named above; each array names one. Nothing has to cross between parts.
Inputs may be any that keep to these rules, and one draw needn't show every extreme that they name: `first_key`: 0 for tokens of the first block; for a token of block b >= 1 a position among the first 128 of block b - 1.
All inputs are finite; a program needn't handle non-finite values.
Results may differ from the reference program's by a relative error of at most 0.0055.
Values may be sent and summed in bfloat16 or wider, within the bound.
No kernel may reach another device: no remote copies, remote signals or barrier semaphores. Data moves between devices by JAX's collectives and lax.ppermute only.
A program may use at most 64 MiB of HBM per device.

```python
import jax
import jax.numpy as jnp
from jax import lax

RANK = 512
BLOCK = 512
H = 8
LAT = 576
TOKENS = 1024


def latent_pair(key):
    base = jnp.clip(jax.random.normal(jax.random.fold_in(key, 101), (TOKENS, LAT), jnp.float32), -6.0, 6.0)
    queries = jnp.clip(jax.random.normal(jax.random.fold_in(key, 105), (TOKENS, H, LAT), jnp.float32), -6.0, 6.0) * 0.5
    bound = 64.0 * 576.0 / LAT
    queries = jnp.clip(queries, -bound, bound)
    return (base, queries)


def draw_latents(key, part):
    return latent_pair(key)[0].astype(jnp.bfloat16)


def draw_queries(key, part):
    return latent_pair(key)[1].astype(jnp.bfloat16)


def draw_first_key(key, part):
    positions = jnp.arange(TOKENS, dtype=jnp.int32)
    group_of = positions // BLOCK
    offsets = jax.random.randint(jax.random.fold_in(key, 201), (TOKENS,), 0, BLOCK // 4, jnp.int32)
    values = jnp.where(group_of >= 1, (group_of - 1) * BLOCK + offsets, 0)
    values = jnp.where(positions == TOKENS - BLOCK, TOKENS - 2 * BLOCK + BLOCK // 4 - 1, values)
    return values.astype(jnp.int32)


def strengthened(result, stream_key, source, target, blocks, factor):
    owner, partner = [(jnp.arange(result.shape[axis_at]) // (result.shape[axis_at] // blocks)).reshape([-1 if axis == axis_at else 1 for axis in range(result.ndim)]) for axis_at in (source, target)]
    chosen = jax.random.permutation(stream_key, blocks)[partner]
    strong = (owner == chosen) | (owner == (partner + blocks // 2) % blocks)
    return jnp.where(strong, factor * result, result)


def steps_of(key, shape, shards, low, top_value):
    def one(axis_at, blocks):
        heights = jax.random.uniform(jax.random.fold_in(jax.random.fold_in(key, 6), axis_at), (blocks,), jnp.float32, low / len(shards), top_value / len(shards))
        return jnp.repeat(jnp.exp(heights), shape[axis_at] // blocks).reshape((-1,) + (1,) * (len(shape) - axis_at - 1))

    gain = one(*shards[0])
    for cut in shards[1:]:
        gain = gain * one(*cut)
    return gain


def bell_draw_with(own_key, dims, scale, most, shards, heavy, kind=jnp.bfloat16):
    drawn = scale * jax.random.normal(own_key, dims, jnp.float32)
    if shards:
        drawn = drawn * steps_of(own_key, dims, shards, -0.22, 0.18)
    return jnp.clip(strengthened(drawn, jax.random.fold_in(own_key, 3), *heavy), -most, most).astype(kind)


def setup_inputs(seed: int = 0, part: int = 0) -> dict:
    streams_of = jax.random.split(jax.random.key(seed), 5)
    part_splits = jax.random.split(jax.random.fold_in(streams_of[4], part), 5)
    queries = draw_queries(jax.random.fold_in(jax.random.fold_in(streams_of[4], part), 71), part)
    latents = draw_latents(jax.random.fold_in(jax.random.fold_in(streams_of[4], part), 71), part)
    out_grad = bell_draw_with(part_splits[2], (TOKENS, H, RANK), 1.0, 6.0, ((0, 2), (1, 8)), (1, 0, 8, 2.0))
    first_key = draw_first_key(jax.random.fold_in(jax.random.fold_in(streams_of[4], part), 71), part)
    return dict(queries=queries, latents=latents, out_grad=out_grad, first_key=first_key)


score_scale = 192.0 ** -0.5


def attend_grads(query_blk, grad_blk, key_rows, visible):
    count, head_count, width = query_blk.shape
    query_rows = query_blk.reshape(count * head_count, width)
    grad_rows = grad_blk.reshape(count * head_count, -1)
    rank_width = grad_rows.shape[1]
    value_rows = key_rows[:, :rank_width]
    scores = jnp.dot(query_rows, key_rows.T, preferred_element_type=jnp.float32) * score_scale
    scores = scores.reshape(count, head_count, -1)
    mask_three = visible[:, None, :]
    row_max = jnp.max(jnp.where(mask_three, scores, -jnp.inf), axis=-1, keepdims=True)
    total = jnp.sum(jnp.where(mask_three, jnp.exp(scores - row_max), 0.0), axis=-1, keepdims=True)
    log_norm = row_max + jnp.log(total)
    attn_probs = jnp.where(mask_three, jnp.exp(scores - log_norm), 0.0).astype(jnp.bfloat16)
    attn_probs = attn_probs.reshape(count * head_count, -1)
    outputs = jnp.dot(attn_probs, value_rows, preferred_element_type=jnp.float32)
    row_delta = jnp.sum(grad_rows.astype(jnp.float32) * outputs, axis=-1, keepdims=True)
    prob_grad = jnp.dot(grad_rows, value_rows.T, preferred_element_type=jnp.float32)
    score_grad = (attn_probs.astype(jnp.float32) * (prob_grad - row_delta) * score_scale).astype(jnp.bfloat16)
    query_grad = jnp.dot(score_grad, key_rows, preferred_element_type=jnp.float32).astype(jnp.bfloat16)
    latent_part = jnp.dot(score_grad.T, query_rows, preferred_element_type=jnp.float32)
    value_part = jnp.dot(attn_probs.T, grad_rows, preferred_element_type=jnp.float32)
    latent_part = jnp.concatenate([latent_part[:, :rank_width] + value_part, latent_part[:, rank_width:]], axis=1)
    return query_grad.reshape(count, head_count, width), latent_part


def reference(queries, latents, out_grad, first_key):
    block_len = BLOCK
    group_total = TOKENS // block_len
    per_step = 8
    steps_count = block_len // per_step
    grad_total = jnp.zeros((TOKENS, LAT), jnp.float32)
    query_parts = []
    for group_id in range(group_total):
        start = group_id * block_len
        own_block = latents[start:start + block_len]
        if group_id > 0:
            prev_block = latents[start - block_len:start]
        else:
            prev_block = jnp.zeros_like(own_block)
        key_rows = jnp.concatenate([prev_block, own_block], axis=0)
        key_pos = (jnp.arange(2 * block_len, dtype=jnp.int32) + (start - block_len)).astype(jnp.int32)
        in_prev = jnp.arange(2 * block_len, dtype=jnp.int32) < block_len
        query_groups = queries[start:start + block_len].reshape(steps_count, per_step, H, LAT)
        grad_groups = out_grad[start:start + block_len].reshape(steps_count, per_step, H, RANK)
        first_groups = first_key[start:start + block_len].reshape(steps_count, per_step)
        pos_groups = (jnp.arange(block_len, dtype=jnp.int32) + start).reshape(steps_count, per_step)

        def scan_step(carry, items):
            query_blk, grad_blk, first_blk, pos_blk = items
            prev_ok = (key_pos[None, :] >= first_blk[:, None]) & (group_id > 0)
            own_ok = key_pos[None, :] <= pos_blk[:, None]
            visible = jnp.where(in_prev[None, :], prev_ok, own_ok)
            query_grad, latent_part = attend_grads(query_blk, grad_blk, key_rows, visible)
            return carry + latent_part, query_grad

        carry_init = jnp.zeros((2 * block_len, LAT), jnp.float32)
        latent_acc, query_blocks = lax.scan(scan_step, carry_init, (query_groups, grad_groups, first_groups, pos_groups))
        query_parts.append(query_blocks.reshape(block_len, H, LAT))
        grad_total = grad_total.at[start:start + block_len].add(latent_acc[block_len:])
        if group_id > 0:
            grad_total = grad_total.at[start - block_len:start].add(latent_acc[:block_len])
    query_grad = jnp.concatenate(query_parts, axis=0)
    return query_grad, grad_total.astype(jnp.bfloat16)
```

```python
import functools

import jax
import jax.numpy as jnp
from jax import lax
from jax.experimental import pallas as pl
from jax.experimental.pallas import tpu as pltpu
from jax.sharding import PartitionSpec as P

score_scale = 192.0 ** (-0.5)
masked_score = -1e30
f32 = jnp.float32
bf16 = jnp.bfloat16


def dot_nn(a, b):
    return lax.dot_general(a, b, (((1,), (0,)), ((), ())), preferred_element_type=f32)


def dot_nt(a, b):
    return lax.dot_general(a, b, (((1,), (1,)), ((), ())), preferred_element_type=f32)


def dot_tn(a, b):
    return lax.dot_general(a, b, (((0,), (0,)), ((), ())), preferred_element_type=f32)


def attend_kernel(pieces, scalars, first_ref, query_ref, grad_ref, *refs):
    own_refs, prev_refs = refs[:pieces], refs[pieces : 2 * pieces]
    prev_out, own_out, score_grad_out, keys_out = refs[2 * pieces : 2 * pieces + 4]
    score_scr, prob_grad_scr, probs_scr = refs[2 * pieces + 4 :]
    block_len = grad_ref.shape[0]
    rank_width = grad_ref.shape[1]
    piece_len = block_len // pieces
    tile = min(256, block_len)
    tiles = block_len // tile
    blk_index = scalars[0]
    group_index = scalars[1]

    for part, piece_refs in ((0, prev_refs), (1, own_refs)):
        for m in range(pieces):
            start = part * block_len + m * piece_len
            keys_out[start : start + piece_len, :] = piece_refs[m][...]

    token_pos = lax.broadcasted_iota(jnp.int32, (1, block_len), 1)

    def visible(c):
        row = lax.broadcasted_iota(jnp.int32, (tile, 1), 0) + (c % tiles) * tile
        key_pos = (blk_index ^ (row // piece_len)) * piece_len + row % piece_len
        if c < tiles:
            return key_pos + (group_index - 1) * block_len >= first_ref[...]
        return key_pos <= token_pos

    def run(chunks):
        rows = {c: pl.ds(c * tile, tile) for c in chunks}
        peak = None
        for c in chunks:
            keys = keys_out[rows[c], :]
            scores = dot_nn(keys, query_ref[...]) * score_scale
            scores = jnp.where(visible(c), scores, masked_score)
            score_scr[rows[c], :] = scores
            top = jnp.max(scores, axis=0, keepdims=True)
            peak = top if peak is None else jnp.maximum(peak, top)
            prob_grad_scr[rows[c], :] = dot_nt(keys[:, :rank_width], grad_ref[...])
        total = 0.0
        for c in chunks:
            lifted = jnp.exp(score_scr[rows[c], :] - peak)
            score_scr[rows[c], :] = lifted
            total = total + jnp.sum(lifted, axis=0, keepdims=True)
        inverse = 1.0 / total
        delta = 0.0
        for c in chunks:
            probs = (score_scr[rows[c], :] * inverse).astype(bf16)
            probs_scr[rows[c], :] = probs
            delta = delta + jnp.sum(
                probs.astype(f32) * prob_grad_scr[rows[c], :], axis=0, keepdims=True
            )
        for c in chunks:
            probs = probs_scr[rows[c], :]
            score_grad = (
                probs.astype(f32) * (prob_grad_scr[rows[c], :] - delta) * score_scale
            ).astype(bf16)
            score_grad_out[rows[c], :] = score_grad
            latent_part = dot_nt(score_grad, query_ref[...])
            value_part = dot_nn(probs, grad_ref[...])
            target = prev_out if c < tiles else own_out
            out_rows = pl.ds((c % tiles) * tile, tile)
            target[out_rows, :rank_width] = (latent_part[:, :rank_width] + value_part).astype(
                target.dtype
            )
            target[out_rows, rank_width:] = latent_part[:, rank_width:].astype(target.dtype)

    @pl.when(group_index > 0)
    def _():
        run(range(2 * tiles))

    @pl.when(group_index == 0)
    def _():
        run(range(tiles, 2 * tiles))
        score_grad_out[:block_len, :] = jnp.zeros((block_len, block_len), bf16)
        prev_out[...] = jnp.zeros(prev_out.shape, prev_out.dtype)


def query_grad_kernel(keys_ref, score_grad_ref, out_ref):
    out_ref[...] = dot_tn(keys_ref[...], score_grad_ref[...]).astype(bf16)


def vmem():
    return pl.BlockSpec(memory_space=pltpu.VMEM)


def attend(scalars, first_row, query_t, grad_rows, own, prev):
    pieces = len(own)
    block_len = grad_rows.shape[0]
    width = query_t.shape[0]
    keys = (2 * block_len, width)
    pairs = (2 * block_len, block_len)
    return pl.pallas_call(
        functools.partial(attend_kernel, pieces),
        out_shape=(
            jax.ShapeDtypeStruct((block_len, width), bf16),
            jax.ShapeDtypeStruct((block_len, width), f32),
            jax.ShapeDtypeStruct(pairs, bf16),
            jax.ShapeDtypeStruct(keys, bf16),
        ),
        in_specs=[pl.BlockSpec(memory_space=pltpu.SMEM)] + [vmem()] * (3 + 2 * pieces),
        out_specs=(vmem(),) * 4,
        scratch_shapes=[pltpu.VMEM(pairs, f32), pltpu.VMEM(pairs, f32), pltpu.VMEM(pairs, bf16)],
        name="attend",
    )(scalars, first_row, query_t, grad_rows, *own, *prev)


def query_grads(keys, score_grad):
    return pl.pallas_call(
        query_grad_kernel,
        out_shape=jax.ShapeDtypeStruct((keys.shape[1], score_grad.shape[1]), bf16),
        in_specs=[vmem(), vmem()],
        out_specs=vmem(),
        name="query_grad",
    )(keys, score_grad)


def shifted(shard, axis, by):
    count = lax.axis_size(axis)
    pairs = [(i, i + by) for i in range(count) if 0 <= i + by < count]
    return lax.ppermute(shard, axis, pairs)


def swapped(shard, mask):
    count = lax.axis_size("blk")
    return lax.ppermute(shard, "blk", [(i, i ^ mask) for i in range(count)])


def gather_pieces(latents, count):
    pieces = [latents] + [None] * (count - 1)
    for m in range(2, count, 2):
        pieces[m] = swapped(latents, m)
    pieces[1] = swapped(latents, 1)
    for m in range(2, count, 2):
        pieces[m + 1] = swapped(pieces[m], 1)
    return pieces


def scatter_pieces(parts, count):
    far = {}
    for m in range(count - 2, -1, -2):
        far[m] = swapped(parts[m + 1].astype(bf16), 1)
    sums = {m: parts[m] + far[m].astype(f32) for m in far}
    total = sums[0]
    for m in range(count - 2, 0, -2):
        total = total + swapped(sums[m].astype(bf16), m).astype(f32)
    return total


def shards(queries, latents, out_grad, first_key):
    block_len, head_local, width = queries.shape
    rank_width = out_grad.shape[2]
    count = lax.axis_size("blk")
    by_swaps = count in (2, 4, 8, 16)
    group_index = lax.axis_index("grp")
    blk_index = lax.axis_index("blk")
    if by_swaps:
        own = gather_pieces(latents, count)
    else:
        own = [lax.all_gather(latents, "blk", axis=0, tiled=True)]
        blk_index = jnp.zeros_like(blk_index)
    prev = [shifted(piece, "grp", 1) for piece in own]
    scalars = jnp.stack([blk_index, group_index]).astype(jnp.int32)
    first_row = first_key.reshape(1, block_len)
    query_parts = []
    own_part = prev_part = None
    for h in range(head_local):
        prev_h, own_h, score_grad, keys = attend(
            scalars, first_row, queries[:, h, :].T, out_grad[:, h, :], own, prev
        )
        query_parts.append((keys, score_grad))
        own_part = own_h if h == 0 else own_part + own_h
        prev_part = prev_h if h == 0 else prev_part.astype(f32) + prev_h.astype(f32)
    from_later = shifted(prev_part.astype(bf16), "grp", -1)
    if by_swaps:
        piece_len = block_len // count
        parts = []
        for m in range(count):
            rows = slice(m * piece_len, (m + 1) * piece_len)
            parts.append(own_part[rows] + from_later[rows].astype(f32))
        latent_total = scatter_pieces(parts, count)
    else:
        latent_total = lax.psum_scatter(
            own_part + from_later.astype(f32), "blk", scatter_dimension=0, tiled=True
        )
    query_grad = jnp.stack([query_grads(k, s).T for k, s in query_parts], axis=1)
    return (query_grad, latent_total.astype(bf16))


def solution(mesh):
    placed = (
        P(("rep", "grp"), "blk", None),
        P(("rep", "grp", "blk"), None),
        P(("rep", "grp"), "blk", None),
        P(("rep", "grp")),
    )
    return jax.shard_map(
        shards,
        mesh=mesh,
        in_specs=placed,
        out_specs=(P(("rep", "grp"), "blk", None), P(("rep", "grp", "blk"), None)),
        check_vma=False,
    )
```

```python
import functools

import jax
import jax.numpy as jnp
from jax import lax
from jax.experimental import pallas as pl
from jax.experimental.pallas import tpu as pltpu
from jax.sharding import PartitionSpec as P


score_scale = 192.0 ** (-0.5)
masked_score = -1e30
most_pieces = 16
kernel_room = 24 * 2**20
f32 = jnp.float32
bf16 = jnp.bfloat16


def dot_nn(a, b):
    return lax.dot_general(a, b, (((1,), (0,)), ((), ())), preferred_element_type=f32)


def dot_nt(a, b):
    return lax.dot_general(a, b, (((1,), (1,)), ((), ())), preferred_element_type=f32)


def dot_tn(a, b):
    return lax.dot_general(a, b, (((0,), (0,)), ((), ())), preferred_element_type=f32)


def tiling(block_len):
    tile = min(256, block_len)
    return tile, block_len // tile


def from_lane(acc, value, lane, op):
    if acc is None:
        return value
    if lane == 0:
        return op(acc, value)
    return jnp.concatenate([acc[:, :lane], op(acc[:, lane:], value)], axis=1)


def place(scalars, ids, refs, keys_ref):
    piece_len = keys_ref.shape[0] // sum(len(i) for i in ids)
    for group, ref in zip(ids, refs):
        for q, m in enumerate(group):
            start = pl.multiple_of((scalars[0] ^ m) * piece_len, piece_len)
            keys_ref[pl.ds(start, piece_len), :] = ref[q * piece_len : (q + 1) * piece_len, :]


def own_kernel(ids, scalars, query_ref, grad_ref, *refs):
    pieces, (keys_ref, score_ref, prob_grad_ref, peak_ref) = refs[:-4], refs[-4:]
    place(scalars, ids, pieces, keys_ref)
    block_len, rank_width = grad_ref.shape
    tile, tiles = tiling(block_len)
    peak = None
    for c in range(tiles):
        rows, lane = pl.ds(c * tile, tile), c * tile
        keys = keys_ref[rows, :]
        scores = dot_nn(keys, query_ref[:, lane:]) * score_scale
        key_pos = lax.broadcasted_iota(jnp.int32, scores.shape, 0)
        token_pos = lax.broadcasted_iota(jnp.int32, scores.shape, 1)
        scores = jnp.where(key_pos <= token_pos, scores, masked_score)
        score_ref[rows, lane:] = scores
        peak = from_lane(peak, jnp.max(scores, axis=0, keepdims=True), lane, jnp.maximum)
        prob_grad_ref[rows, lane:] = dot_nt(keys[:, :rank_width], grad_ref[lane:, :])
    peak_ref[...] = peak


def joint_kernel(ids, scalars, first_ref, query_ref, grad_ref, own_score_ref, own_prob_grad_ref,
                 own_peak_ref, *refs):
    pieces = refs[: len(ids)]
    (keys_ref, prev_ref, prev_sg_ref, own_sg_ref, own_probs_ref, prev_score_ref,
     prev_prob_grad_ref, prev_probs_ref) = refs[len(ids) :]
    block_len, rank_width = grad_ref.shape
    tile, tiles = tiling(block_len)

    def run(with_prev):
        parts = []
        if with_prev:
            for c in range(tiles):
                parts.append((pl.ds(c * tile, tile), 0, prev_score_ref, prev_prob_grad_ref,
                              prev_probs_ref, prev_sg_ref))
        for c in range(tiles):
            parts.append((pl.ds(c * tile, tile), c * tile, own_score_ref, own_prob_grad_ref,
                          own_probs_ref, own_sg_ref))
        peak = own_peak_ref[...]
        if with_prev:
            place(scalars, ids, pieces, keys_ref)
            first = first_ref[...] - (scalars[1] - 1) * block_len
            for c in range(tiles):
                rows = pl.ds(c * tile, tile)
                keys = keys_ref[rows, :]
                scores = dot_nn(keys, query_ref[...]) * score_scale
                key_pos = lax.broadcasted_iota(jnp.int32, scores.shape, 0) + c * tile
                scores = jnp.where(key_pos >= first, scores, masked_score)
                prev_score_ref[rows, :] = scores
                peak = jnp.maximum(peak, jnp.max(scores, axis=0, keepdims=True))
                prev_prob_grad_ref[rows, :] = dot_nt(keys[:, :rank_width], grad_ref[...])
        total = None
        for rows, lane, score_ref, _, _, _ in parts:
            lifted = jnp.exp(score_ref[rows, lane:] - peak[:, lane:])
            score_ref[rows, lane:] = lifted
            total = from_lane(total, jnp.sum(lifted, axis=0, keepdims=True), lane, jnp.add)
        inverse = 1.0 / total
        delta = None
        for rows, lane, score_ref, prob_grad_ref, probs_ref, _ in parts:
            probs = (score_ref[rows, lane:] * inverse[:, lane:]).astype(bf16)
            probs_ref[rows, lane:] = probs
            term = jnp.sum(probs.astype(f32) * prob_grad_ref[rows, lane:], axis=0, keepdims=True)
            delta = from_lane(delta, term, lane, jnp.add)
        for rows, lane, _, prob_grad_ref, probs_ref, sg_ref in parts:
            probs = probs_ref[rows, lane:].astype(f32)
            sg = probs * (prob_grad_ref[rows, lane:] - delta[:, lane:]) * score_scale
            sg_ref[rows, lane:] = sg.astype(bf16)
        if with_prev:
            for c in range(tiles):
                rows = pl.ds(c * tile, tile)
                store_latents(prev_ref, rows, prev_sg_ref[rows, :], prev_probs_ref[rows, :],
                              query_ref[...], grad_ref[...])
        else:
            prev_ref[...] = jnp.zeros(prev_ref.shape, prev_ref.dtype)

    @pl.when(scalars[1] > 0)
    def _():
        run(True)

    @pl.when(scalars[1] == 0)
    def _():
        run(False)


def store_latents(out_ref, rows, score_grad, probs, query_t, grad_rows):
    width, rank_width = query_t.shape[0], grad_rows.shape[1]
    latent_part = dot_nt(score_grad, query_t)
    value_part = dot_nn(probs, grad_rows)
    out_ref[rows, :rank_width] = (latent_part[:, :rank_width] + value_part).astype(out_ref.dtype)
    rest = latent_part[:, rank_width:]
    pad = out_ref.shape[1] - width
    if pad:
        rest = jnp.concatenate([rest, jnp.zeros((rest.shape[0], pad), f32)], axis=1)
    out_ref[rows, rank_width:] = rest.astype(out_ref.dtype)


def own_latents_kernel(query_ref, grad_ref, own_sg_ref, own_probs_ref, out_ref):
    tile, tiles = tiling(grad_ref.shape[0])
    for c in range(tiles):
        rows, lane = pl.ds(c * tile, tile), c * tile
        store_latents(out_ref, rows, own_sg_ref[rows, lane:], own_probs_ref[rows, lane:],
                      query_ref[:, lane:], grad_ref[lane:, :])


def chunks_kernel(groups, scalars, own_ref, later_ref, *outs):
    piece_len = own_ref.shape[0] // len(outs)

    def run(with_later):
        for m, out in enumerate(outs):
            start = pl.multiple_of((scalars[0] ^ m) * piece_len, piece_len)
            rows = own_ref[pl.ds(start, piece_len), :]
            if with_later:
                rows = rows + later_ref[pl.ds(start, piece_len), :].astype(f32)
            out[...] = rows.astype(out.dtype)

    @pl.when(scalars[1] < groups - 1)
    def _():
        run(True)

    @pl.when(scalars[1] == groups - 1)
    def _():
        run(False)


def query_grad_kernel(scalars, prev_keys_ref, own_keys_ref, prev_sg_ref, own_sg_ref, out_ref):
    tile, tiles = tiling(own_sg_ref.shape[0])

    def run(with_prev):
        for c in range(tiles):
            lanes = slice(c * tile, (c + 1) * tile)
            seen = (c + 1) * tile
            acc = dot_tn(own_keys_ref[:seen, :], own_sg_ref[:seen, lanes])
            if with_prev:
                acc = acc + dot_tn(prev_keys_ref[...], prev_sg_ref[:, lanes])
            out_ref[:, lanes] = acc.astype(bf16)

    @pl.when(scalars[1] > 0)
    def _():
        run(True)

    @pl.when(scalars[1] == 0)
    def _():
        run(False)


def add_kernel(*refs):
    total = refs[0][...].astype(f32)
    for ref in refs[1:-1]:
        total = total + ref[...].astype(f32)
    out_ref = refs[-1]
    out_ref[...] = total[:, : out_ref.shape[1]].astype(bf16)


def added(terms, width=None):
    rows, cols = terms[0].shape
    return call(add_kernel, [((rows, width or cols), bf16)], terms)[0]


def on_chip(x):
    return pltpu.with_memory_space_constraint(x, pltpu.VMEM)


def call(kernel, outs, args, scratch=(), scalars=None):
    specs = [pl.BlockSpec(memory_space=pltpu.VMEM)] * len(args)
    args = [on_chip(x) for x in args]
    if scalars is not None:
        specs = [pl.BlockSpec(memory_space=pltpu.SMEM)] + specs
        args = [scalars] + args
    result = pl.pallas_call(
        kernel,
        out_shape=tuple(pltpu.VMEM(s, d) for s, d in outs),
        in_specs=specs,
        out_specs=tuple(pl.BlockSpec(memory_space=pltpu.VMEM) for _ in outs),
        scratch_shapes=[pltpu.VMEM(s, d) for s, d in scratch],
        compiler_params=pltpu.CompilerParams(vmem_limit_bytes=kernel_room),
    )(*args)
    return result


def rotated(shard, axis, by):
    count = lax.axis_size(axis)
    return lax.ppermute(shard, axis, [(i, (i + by) % count) for i in range(count)])


def swapped(shard, mask):
    count = lax.axis_size("blk")
    return lax.ppermute(shard, "blk", [(i, i ^ mask) for i in range(count)])


def top_bit(m):
    return 1 << (m.bit_length() - 1)


def routes(count):
    direct = [m for m in range(2, count) if m == top_bit(m)] + [1]
    relayed = [m for m in range(1, count) if m != top_bit(m)]
    relayed.sort(key=lambda m: (top_bit(m), -((m - top_bit(m)) & 1), -m))
    return direct, relayed


def shards(queries, latents, out_grad, first_key):
    block_len, head_local, width = queries.shape
    count = lax.axis_size("blk")
    groups = lax.axis_size("grp")
    by_swaps = routed(count)
    blk_index = lax.axis_index("blk") if by_swaps else jnp.zeros((), jnp.int32)
    scalars = jnp.stack([blk_index, lax.axis_index("grp")]).astype(jnp.int32)
    padded = -(-width // 128) * 128
    first_row = first_key.reshape(1, block_len)

    if by_swaps:
        direct, relayed = routes(count)
        pieces = {0: latents}
        for m in direct:
            pieces[m] = swapped(latents, m)
        early = [0] + direct
        prev_early = rotated(jnp.concatenate([pieces[m] for m in early], axis=0), "grp", 1)
        for m in relayed:
            pieces[m] = swapped(pieces[top_bit(m)], m - top_bit(m))
        prev_late = rotated(jnp.concatenate([pieces[m] for m in relayed], axis=0), "grp", 1)
        own_ids = tuple((m,) for m in range(count))
        own = [pieces[m] for m in range(count)]
        prev_ids = (tuple(early), tuple(relayed))
        prev = [prev_early, prev_late]
    else:
        own_ids = prev_ids = ((0,),)
        own = [lax.all_gather(latents, "blk", axis=0, tiled=True)]
        prev = [rotated(own[0], "grp", 1)]

    square = (block_len, block_len)
    query_work = []
    own_part = prev_part = None
    for h in range(head_local):
        query_t, grad_rows = queries[:, h, :].T, out_grad[:, h, :]
        own_keys, own_score, own_prob_grad, own_peak = call(
            functools.partial(own_kernel, own_ids),
            [((block_len, width), bf16), (square, f32), (square, f32), ((1, block_len), f32)],
            [query_t, grad_rows] + own, scalars=scalars,
        )
        prev_keys, prev_h, prev_sg, own_sg, own_probs = call(
            functools.partial(joint_kernel, prev_ids),
            [((block_len, width), bf16), ((block_len, padded), bf16), (square, bf16),
             (square, bf16), (square, bf16)],
            [first_row, query_t, grad_rows, own_score, own_prob_grad, own_peak] + prev,
            scratch=[(square, f32), (square, f32), (square, bf16)], scalars=scalars,
        )
        (own_h,) = call(own_latents_kernel, [((block_len, padded), f32)],
                        [query_t, grad_rows, own_sg, own_probs])
        query_work.append((prev_keys, own_keys, prev_sg, own_sg))
        own_part = own_h if h == 0 else own_part + own_h
        prev_part = prev_h if h == 0 else prev_part.astype(f32) + prev_h.astype(f32)
    later = rotated(prev_part.astype(bf16), "grp", -1)

    pieces_out = count if by_swaps else 1
    piece = (block_len // pieces_out, padded)
    kinds = [f32 if m == 0 or m == top_bit(m) and m > 1 else bf16 for m in range(pieces_out)]
    chunks = call(functools.partial(chunks_kernel, groups),
                  [(piece, kind) for kind in kinds], [own_part, later], scalars=scalars)
    if by_swaps:
        sums = {m: [chunks[m]] for m in direct}
        for m in sorted(relayed, key=lambda m: (-top_bit(m), -(m - top_bit(m) & 1), -m)):
            sums[top_bit(m)].append(swapped(chunks[m], m - top_bit(m)))
        last = [chunks[0]]
        for m in direct:
            sent = chunks[m] if len(sums[m]) == 1 else added(sums[m])
            last.append(swapped(sent, m))
        total = added(last, width)
    else:
        total = lax.psum_scatter(chunks[0], "blk", scatter_dimension=0, tiled=True)
        total = total[:, :width].astype(bf16)
    query_parts = [
        call(query_grad_kernel, [((width, block_len), bf16)], list(work),
             scalars=scalars)[0].T
        for work in query_work
    ]
    return (jnp.stack(query_parts, axis=1), total)


def routed(count):
    return 2 <= count <= most_pieces and count & (count - 1) == 0


def solution(mesh):
    placed = (
        P(("rep", "grp"), "blk", None),
        P(("rep", "grp", "blk"), None),
        P(("rep", "grp"), "blk", None),
        P(("rep", "grp")),
    )

    return jax.shard_map(
        shards,
        mesh=mesh,
        in_specs=placed,
        out_specs=(P(("rep", "grp"), "blk", None), P(("rep", "grp", "blk"), None)),
        check_vma=False,
    )
```
